128 devices in a mesh: branch: 4 (over x), seq: 32 (over z, y, core).
Axes of the slice: x: 4, y: 4, z: 4, core: 2. Of those that a mesh axis runs over, the one named last changes fastest.
Arguments:
- query: bfloat16 [4, 4096, 8192], P('branch', 'seq'), may hold values from -150 to 150
- key_new: bfloat16 [4, 4096, 1024], P('branch', 'seq'), may hold values from -6 to 6
- value_new: bfloat16 [4, 4096, 1024], P('branch', 'seq'), may hold values from -18 to 18
- hist_key: bfloat16 [512, 1024], P('seq'), may hold values from -6 to 6
- hist_value: bfloat16 [512, 1024], P('seq'), may hold values from -18 to 18
- sib_source: int32 [4, 4], replicated, may hold values from 0 to 3, as said below
- sib_block: int32 [4, 4], replicated, may hold values from 0 to 15, as said below
- sib_mask: int32 [4, 16, 4], replicated, may hold values 0 or 1
Outputs:
- attended: bfloat16 [4, 4096, 8192], P('branch', 'seq')
The draws below stay inside these ranges and needn't reach their ends.
Inputs may be any that keep to these rules, and one draw needn't show every extreme that they name: `sib_source`: never the reader itself. In every reader's list exactly 2 slots name one source and no source is named more than 2 times. `sib_block`: A reader lists no block of one source twice.
All inputs are finite; a program needn't handle non-finite values.
Results may differ from the reference program's by a relative error of at most 0.0036.
Values may be sent and summed in bfloat16 or wider, within the bound.
No kernel may reach another device: no remote copies, remote signals or barrier semaphores. Data moves between devices by JAX's collectives and lax.ppermute only.
A program may use at most 128 MiB of HBM per device.

```python
import math
import jax
import jax.numpy as jnp
from jax import lax

QH = 64
KVH = 8
HD = 128
BLOCK = 256
NSIB = 4
SRCMAX = 2
BRANCHES = 4
OWN_LEN = 4096
HIST = 512
NBLK = 16


def history_base(key):
    raw = jax.random.normal(jax.random.fold_in(key, 7), (HIST, KVH * HD), jnp.float32)
    raw = jnp.clip(raw, -6.0, 6.0)
    return raw


def draw_hist_key(key, part):
    return history_base(key).astype(jnp.bfloat16)


def draw_query(key, part):
    base = jax.random.normal(jax.random.fold_in(key, 13), (BRANCHES, OWN_LEN, QH * HD), jnp.float32)
    base = jnp.clip(2.0 * base, -12.0, 12.0)
    return base.astype(jnp.bfloat16)


def sibling_lists(key):
    base = jax.random.fold_in(key, 31)
    heavy = jax.random.randint(jax.random.fold_in(base, 1), (BRANCHES,), 1, 4)
    second = jnp.where(heavy == 1, 2, 1)
    third = jnp.where(heavy == 3, 2, 3)
    split = jax.random.randint(jax.random.fold_in(base, 2), (BRANCHES,), 0, SRCMAX)
    slots = jnp.arange(NSIB, dtype=jnp.int32)[None, :]
    offset = jnp.where(slots < SRCMAX, heavy[:, None], jnp.where(slots < SRCMAX + split[:, None], second[:, None], third[:, None]))
    within = jnp.where(slots < SRCMAX, slots, jnp.where(slots < SRCMAX + split[:, None], slots - SRCMAX, slots - SRCMAX - split[:, None]))

    def one_order(order_key):
        return jax.random.permutation(order_key, NBLK)
    orders = jax.vmap(one_order)(jax.random.split(jax.random.fold_in(base, 3), BRANCHES * 3)).reshape(BRANCHES, 3, NBLK)
    readers = jnp.arange(BRANCHES, dtype=jnp.int32)[:, None]
    blocks = orders[readers, offset - 1, within]
    sources = (readers + offset) % BRANCHES

    def one_shuffle(order_key):
        return jax.random.permutation(order_key, NSIB)
    shuffle = jax.vmap(one_shuffle)(jax.random.split(jax.random.fold_in(base, 4), BRANCHES))
    sources = jnp.take_along_axis(sources, shuffle, axis=1)
    blocks = jnp.take_along_axis(blocks, shuffle, axis=1)
    return (sources.astype(jnp.int32), blocks.astype(jnp.int32))


def draw_sib_source(key, part):
    return sibling_lists(key)[0]


def draw_sib_block(key, part):
    return sibling_lists(key)[1]


def place_ends(values, rng, smallest, high):
    extent = values.shape
    index_at = [jax.random.randint(jax.random.fold_in(rng, axis), (), 0, extent[axis]) for axis in range(len(extent))]
    values = values.at[tuple(index_at)].set(smallest)
    longest = extent.index(max(extent))
    index_at[longest] = (index_at[longest] + 1) % extent[longest]
    return values.at[tuple(index_at)].set(high)


def block_scale(key, shape, pieces, low, high):
    gain = 1.0
    for axis_at, blocks in pieces:
        draws = jax.random.uniform(jax.random.fold_in(jax.random.fold_in(key, 6), axis_at), (blocks,), jnp.float32, low / len(pieces), high / len(pieces))
        gain = gain * jnp.repeat(jnp.exp(draws), shape[axis_at] // blocks).reshape((-1,) + (1,) * (len(shape) - 1 - axis_at))
    return gain


def normal_values(stream_key, extent, deviation, limit, shards=(), kind=jnp.bfloat16):
    drawn = deviation * jax.random.normal(stream_key, extent, jnp.float32)
    if shards:
        drawn = drawn * block_scale(stream_key, extent, shards, -0.22, 0.18)
    return jnp.clip(drawn, -limit, limit).astype(kind)


def setup_inputs(seed: int = 0) -> dict:
    streams_of = jax.random.split(jax.random.key(seed), 9)
    return {
        "query": draw_query(jax.random.fold_in(streams_of[8], 71), 0),
        "key_new": normal_values(streams_of[1], (BRANCHES, OWN_LEN, KVH * HD), 1.0, 6.0, ((0, 4), (1, 32))),
        "value_new": normal_values(streams_of[2], (BRANCHES, OWN_LEN, KVH * HD), 3.0, 18.0, ((0, 4), (1, 32))),
        "hist_key": draw_hist_key(jax.random.fold_in(streams_of[8], 71), 0),
        "hist_value": normal_values(streams_of[4], (HIST, KVH * HD), 3.0, 18.0, ((0, 32),)),
        "sib_source": draw_sib_source(jax.random.fold_in(streams_of[8], 71), 0),
        "sib_block": draw_sib_block(jax.random.fold_in(streams_of[8], 71), 0),
        "sib_mask": place_ends((jax.random.randint(streams_of[7], (BRANCHES, NBLK, NSIB), 0, 2) < 1).astype(jnp.int32), jax.random.fold_in(streams_of[7], 1), 0, 1),
    }


def visibility(first_row, tile_rows, mask_rows):
    positions = first_row + jnp.arange(tile_rows, dtype=jnp.int32)
    past = jnp.ones((tile_rows, HIST), dtype=jnp.bool_)
    causal = jnp.arange(OWN_LEN, dtype=jnp.int32)[None, :] <= positions[:, None]
    listed = jnp.repeat(mask_rows[positions // BLOCK] == 1, BLOCK, axis=1)
    return jnp.concatenate([past, causal, listed], axis=1)

def reference(query, key_new, value_new, hist_key, hist_value, sib_source, sib_block, sib_mask):
    group_size = QH // KVH
    tile_rows = min(512, OWN_LEN)
    tile_count = OWN_LEN // tile_rows
    score_scale = 1.0 / math.sqrt(HD)
    key_blocks = key_new.reshape(BRANCHES, NBLK, BLOCK, KVH, HD)
    value_blocks = value_new.reshape(BRANCHES, NBLK, BLOCK, KVH, HD)
    results = []
    for branch in range(BRANCHES):
        listed_k = key_blocks[sib_source[branch], sib_block[branch]].reshape(NSIB * BLOCK, KVH, HD)
        listed_v = value_blocks[sib_source[branch], sib_block[branch]].reshape(NSIB * BLOCK, KVH, HD)
        all_keys = jnp.concatenate([hist_key.reshape(HIST, KVH, HD), key_new[branch].reshape(OWN_LEN, KVH, HD), listed_k], 0).transpose(1, 0, 2)
        all_values = jnp.concatenate([hist_value.reshape(HIST, KVH, HD), value_new[branch].reshape(OWN_LEN, KVH, HD), listed_v], 0).transpose(1, 0, 2)
        queries = query[branch].reshape(OWN_LEN, KVH, group_size, HD).transpose(1, 0, 2, 3)
        mask_rows = sib_mask[branch]

        def per_head(operands):
            head_q, head_k, head_v = operands
            key_float = head_k.astype(jnp.float32)
            value_float = head_v.astype(jnp.float32)

            def per_tile(tile_index):
                first_row = tile_index * tile_rows
                tile_q = lax.dynamic_slice_in_dim(head_q, first_row, tile_rows, 0).astype(jnp.float32)
                scores = jnp.einsum('tgd,kd->gtk', tile_q, key_float) * score_scale
                visible = visibility(first_row, tile_rows, mask_rows)
                scores = jnp.where(visible[None], scores, -jnp.inf)
                largest = lax.optimization_barrier(jnp.max(scores, axis=-1, keepdims=True))
                weights = jnp.exp(scores - largest)
                weight_total = lax.optimization_barrier(jnp.sum(weights, axis=-1))
                weight_bf = lax.optimization_barrier(weights.astype(jnp.bfloat16))
                weighted = jnp.einsum('gtk,kd->tgd', weight_bf.astype(jnp.float32), value_float)
                return (weighted / weight_total.T[:, :, None]).astype(jnp.bfloat16)
            tiles = lax.map(per_tile, jnp.arange(tile_count, dtype=jnp.int32))
            return tiles.reshape(OWN_LEN, group_size, HD)
        heads_out = lax.map(per_head, (queries, all_keys, all_values))
        results.append(heads_out.transpose(1, 0, 2, 3).reshape(OWN_LEN, QH * HD))
    return jnp.stack(results)
```

```python
import math

import jax
import jax.numpy as jnp
from jax import lax
from jax.experimental import pallas as pl
from jax.experimental.pallas import tpu as pltpu
from jax.sharding import Mesh
from jax.sharding import PartitionSpec as P

KVH = 8
HD = 128
BLOCK = 256
NSIB = 4
SRCMAX = 2
TOK = 128
GROUP = 1024
QW = 512
Z, Y, CORE = "seq_0", "seq_1", "seq_2"
EXP2_SCALE = math.log2(math.e) / math.sqrt(HD)
HIDDEN = -1e30
CALLS = ((2, 3), (6, 7), (4, 5), (1, 0))


def attend_kernel(plan, q0, q1, hist, own0, own1, own2, own3, sib, out0, out1, q_t, acc, top):
    step = pl.program_id(0)
    chunk_z = plan[0, step]
    chunk_core = plan[1, step]
    reader_y = plan[2, step]
    owns = (own0, own1, own2, own3)

    def load(ref):
        for h in range(KVH):
            q_t[:, h * HD : (h + 1) * HD] = ref[:, h * HD : (h + 1) * HD].T

    @pl.when(step == 0)
    def _():
        load(q0)

    @pl.when(step == 1)
    def _():
        load(q1)

    def block(keys, values_t, visible=None, first=False):
        rows = keys.shape[0]
        row = lax.broadcasted_iota(jnp.int32, (16, rows), 0)
        ones = jnp.where(row == 0, 1.0, 0.0).astype(jnp.bfloat16)
        values_t = jnp.concatenate([values_t, ones], axis=0)
        old = None if first else top[...]
        held = {}
        tops = []
        count = GROUP // QW

        def score(g):
            held[g] = lax.dot_general(
                keys,
                q_t[:, g * QW : (g + 1) * QW],
                (((1,), (0,)), ((), ())),
                preferred_element_type=jnp.float32,
            )

        def weigh(g):
            s = held[g]
            if visible is not None:
                s = jnp.where(visible, s, HIDDEN)
            peak = jnp.max(s, axis=0, keepdims=True) * EXP2_SCALE
            shrink = None
            if not first:
                before = old[:, g * QW : (g + 1) * QW]
                peak = jnp.maximum(before, peak)
                shrink = jnp.exp2(before - peak)
            tops.append(peak)
            held[g] = (jnp.exp2(s * EXP2_SCALE - peak).astype(jnp.bfloat16), shrink)

        def gather(g):
            weights, shrink = held[g]
            cols = slice(g * QW, (g + 1) * QW)
            part = lax.dot_general(
                values_t, weights, (((1,), (0,)), ((), ())), preferred_element_type=jnp.float32
            )
            acc[:, cols] = part if first else acc[:, cols] * shrink + part

        for t in range(count + 2):
            if t < count:
                score(t)
            if 0 <= t - 1 < count:
                weigh(t - 1)
            if 0 <= t - 2 < count:
                gather(t - 2)
        top[...] = jnp.concatenate(tops, axis=1)

    def tiles(pieces):
        keys = jnp.concatenate([p[0] for p in pieces], axis=0)
        values_t = jnp.concatenate([p[1] for p in pieces], axis=1)
        return keys, values_t

    block(*tiles([hist[t] for t in range(4)]), first=True)

    def past(z, carry):
        for pair in (owns[:2], owns[2:]):
            block(*tiles([own[2 * z + c] for own in pair for c in range(2)]))
        return carry

    lax.fori_loop(0, chunk_z, past, 0)

    key_row = lax.broadcasted_iota(jnp.int32, (2 * TOK, QW), 0)
    query_col = lax.broadcasted_iota(jnp.int32, (2 * TOK, QW), 1) % TOK + chunk_core * TOK
    block(*tiles([own0[2 * chunk_z + c] for c in range(2)]), visible=key_row <= query_col)
    for r in range(1, 4):

        @pl.when(reader_y >= r)
        def _():
            source = owns[r]
            block(*tiles([source[2 * chunk_z + c] for c in range(2)]))

    def listed(slot, carry):
        @pl.when(plan[3 + slot, step] == 1)
        def _():
            where = [lax.rem(reader_y + 4 - t, 4) for t in range(4)]
            keys = jnp.concatenate([sib[where[0], slot], sib[where[1], slot]], axis=0)
            values_t = jnp.concatenate([sib[where[2], slot], sib[where[3], slot]], axis=1)
            block(keys, values_t)

        return carry

    lax.fori_loop(0, NSIB, listed, 0)

    def store(ref):
        for h in range(KVH):
            cols = slice(h * HD, (h + 1) * HD)
            ref[:, cols] = (acc[0:HD, cols] / acc[HD : HD + 1, cols]).T.astype(jnp.bfloat16)

    @pl.when(step == 0)
    def _():
        store(out0)

    @pl.when(step == 1)
    def _():
        store(out1)


def attend(plan, q0, q1, hist, owns, sib):
    def whole(a):
        return pl.BlockSpec(a.shape, lambda i, plan: (0,) * a.ndim, pipeline_mode=pl.Buffered(1))

    operands = (q0, q1, hist, *owns, sib)
    chunk = jax.ShapeDtypeStruct((TOK, GROUP), jnp.bfloat16)
    return pl.pallas_call(
        attend_kernel,
        out_shape=(chunk, chunk),
        grid_spec=pltpu.PrefetchScalarGridSpec(
            num_scalar_prefetch=1,
            grid=(2,),
            in_specs=[whole(a) for a in operands],
            out_specs=[pl.BlockSpec((TOK, GROUP), lambda i, plan: (0, 0))] * 2,
            scratch_shapes=[
                pltpu.VMEM((HD, GROUP), jnp.bfloat16),
                pltpu.VMEM((HD + 16, GROUP), jnp.float32),
                pltpu.VMEM((1, GROUP), jnp.float32),
            ],
        ),
        compiler_params=pltpu.CompilerParams(vmem_limit_bytes=32 * 2**20),
    )(plan, *operands)


def shifted(value, axis, by):
    n = lax.axis_size(axis)
    return lax.ppermute(value, axis, [(k, (k + by) % n) for k in range(n)])


def exchanged(value, step):
    return lax.ppermute(value, (Z, CORE), [(k, k ^ step) for k in range(8)])


def key_value_tiles(keys, values):
    rows = keys.shape[0]
    k = keys.reshape(rows, KVH, HD).transpose(1, 0, 2)
    v = values.reshape(rows, KVH, HD).transpose(1, 2, 0)
    return k, v


def body(query, key_new, value_new, hist_key, hist_value, sib_source, sib_block, sib_mask):
    z, y, core = lax.axis_index(Z), lax.axis_index(Y), lax.axis_index(CORE)
    me = z * 2 + core
    reader = lax.axis_index("branch")

    k, v = key_value_tiles(key_new[0], value_new[0])
    own = lax.all_to_all(jnp.stack([k, v], axis=1), (Z, CORE), split_axis=0, concat_axis=0, tiled=True)
    past = jnp.stack(
        [hist_key.reshape(16, KVH, HD).transpose(1, 0, 2), hist_value.reshape(16, KVH, HD).transpose(1, 0, 2)], axis=1
    )
    past = lax.all_to_all(past, (Z, CORE), split_axis=0, concat_axis=0, tiled=True)

    up, down = shifted(own, Y, 1), shifted(own, Y, -1)
    over = jnp.concatenate([shifted(up[:4], Y, 1), shifted(down[4:], Y, -1)], axis=0)
    owns = (own, up, over, down)
    past_all = jnp.stack([past, shifted(past, Y, 1), shifted(past, Y, 2), shifted(past, Y, -1)])
    past_k = past_all[:, :, 0].reshape(4, TOK, HD)
    past_v = past_all[:, :, 1].reshape(4, TOK, HD).transpose(0, 2, 1)
    hist = jnp.stack([past_k, past_v], axis=1)

    q_cols = query[0]
    queries = {}
    for pair in CALLS:
        for s in pair:
            piece = lax.dynamic_slice_in_dim(q_cols, (me ^ s) * GROUP, GROUP, 1)
            queries[s] = exchanged(piece, s) if s else piece

    tile_core, tile_kind = y % 2, y // 2
    mine = jnp.stack(
        [
            lax.dynamic_index_in_dim(
                lax.dynamic_index_in_dim(o.reshape(4, 2, 2, HD, HD), tile_kind, 2, keepdims=False),
                tile_core,
                1,
                keepdims=False,
            )
            for o in owns
        ]
    )
    my_source = lax.dynamic_index_in_dim(sib_source, reader, 0, keepdims=False)
    my_mask = lax.dynamic_index_in_dim(sib_mask, reader, 0, keepdims=False)
    from_me = sib_source == reader
    sender_rank = jnp.cumsum(from_me.astype(jnp.int32), axis=1) - 1
    slot_hit = from_me[:, :, None] & (
        sender_rank[:, :, None] == jnp.arange(SRCMAX, dtype=jnp.int32)[None, None, :]
    )
    send_table = jnp.sum(jnp.where(slot_hit, sib_block[:, :, None], 0), axis=1)
    place = ((y - send_table) % 4) * 4 + send_table // 4
    sent = mine.reshape(16, HD, HD)[place]
    got = lax.all_to_all(sent, "branch", split_axis=0, concat_axis=0, tiled=True)
    slots = jnp.arange(NSIB, dtype=jnp.int32)
    same = (my_source[None, :] == my_source[:, None]) & (slots[None, :] < slots[:, None])
    rank = jnp.sum(same.astype(jnp.int32), axis=1)
    listed = got.reshape(-1, HD, HD)[my_source * SRCMAX + rank]
    sib = jnp.stack([listed, shifted(listed, Y, 1), shifted(listed, Y, 2), shifted(listed, Y, -1)])

    parts = {}
    for pair in CALLS:
        chunks = jnp.stack([me ^ s for s in pair])
        visible = my_mask[(chunks // 2) * 4 + y]
        plan = jnp.concatenate(
            [(chunks // 2)[None], (chunks % 2)[None], jnp.broadcast_to(y, (1, 2)), visible.T], axis=0
        ).astype(jnp.int32)
        results = attend(plan, queries[pair[0]], queries[pair[1]], hist, owns, sib)
        for s, result in zip(pair, results):
            parts[s] = exchanged(result, s) if s else result
    out = jnp.zeros((TOK, KVH * GROUP), jnp.bfloat16)
    for s in range(8):
        out = lax.dynamic_update_slice_in_dim(out, parts[s], (me ^ s) * GROUP, 1)
    return out[None]


def solution(mesh):
    split = Mesh(
        mesh.devices.reshape(mesh.shape["branch"], 4, 4, 2), ("branch", Z, Y, CORE)
    )
    seq = (Z, Y, CORE)
    placed = (
        P("branch", seq, None),
        P("branch", seq, None),
        P("branch", seq, None),
        P(seq, None),
        P(seq, None),
        P(),
        P(),
        P(),
    )
    return jax.shard_map(
        body, mesh=split, in_specs=placed, out_specs=P("branch", seq, None), check_vma=False
    )
```

```python
import math

import jax
import jax.numpy as jnp
from jax import lax
from jax.experimental import pallas as pl
from jax.experimental.pallas import tpu as pltpu
from jax.sharding import Mesh
from jax.sharding import PartitionSpec as P


KVH = 8
HD = 128
NSIB = 4
SRCMAX = 2
TOK = 128
PAST = 16
GROUP = 1024
Z, Y, CORE = "seq_0", "seq_1", "seq_2"
EXP2_SCALE = math.log2(math.e) / math.sqrt(HD)
HIDDEN = -1e30
OWN0, SIB0, DUMMY = 4, 36, 44
VROWS = HD + 16
SPAN = 8
QW = 512
HALVES = GROUP // QW
KB = SPAN * TOK


def make_kernel(kind, chunks):
    has_own, has_sib = kind != "close", kind != "open"

    def kernel(plan, *refs):
        refs = list(refs)

        def take(count):
            taken = refs[:count]
            del refs[:count]
            return taken

        queries = take(chunks)
        states = take(chunks) if kind == "close" else []
        owns = take(4) if has_own else []
        sibs = take(1) if has_sib else []
        outs = take(chunks)
        kbuf, vbuf, past, todo, q_t, s_buf, p_buf, a_buf, acc, top, sem = refs
        step = pl.program_id(0)
        chunk_z, chunk_core, y = plan[0, step], plan[1, step], plan[2, step]

        @pl.when(step == 0)
        def _():
            pairs = []
            for r, own in enumerate(owns):
                here = pl.ds(OWN0 + 8 * r, 8)
                pairs.append((own.at[:, pl.ds(0, TOK)], kbuf.at[here]))
                pairs.append((own.at[:, pl.ds(TOK, HD)], vbuf.at[here, pl.ds(0, HD)]))
                pairs.append((own.at[:, pl.ds(TOK + HD, 2 * PAST)], past.at[r]))
            for t in range(4 if has_sib else 0):
                source = sibs[0].at[lax.rem(y + 4 - t, 4)]
                here = pl.ds(SIB0 + 4 * (t % 2), 4)
                pairs.append((source, kbuf.at[here] if t < 2 else vbuf.at[here, pl.ds(0, HD)]))
            copies = [pltpu.make_async_copy(a, b, sem.at[i]) for i, (a, b) in enumerate(pairs)]
            for copy in copies:
                copy.start()
            row = lax.broadcasted_iota(jnp.int32, (VROWS - HD, TOK), 0)
            ones = jnp.where(row == 0, 1.0, 0.0).astype(jnp.bfloat16)
            for t in range(DUMMY):
                vbuf[t, HD:VROWS, :] = ones
            vbuf[DUMMY] = jnp.zeros((VROWS, TOK), jnp.bfloat16)
            for copy in copies:
                copy.wait()
            for r in range(len(owns)):
                kbuf[r] = past[r, :, 0:PAST].reshape(TOK, HD)
                vbuf[r, 0:HD] = past[r, :, PAST : 2 * PAST].reshape(TOK, HD).T

        def load(ref):
            for h in range(KVH):
                cols = slice(h * HD, (h + 1) * HD)
                scaled = ref[:, cols].T.astype(jnp.float32) * EXP2_SCALE
                upper = scaled.astype(jnp.bfloat16)
                q_t[0:HD, cols] = upper
                q_t[HD : 2 * HD, cols] = (scaled - upper.astype(jnp.float32)).astype(jnp.bfloat16)

        for i in range(chunks):

            @pl.when(step == i)
            def _(i=i):
                load(queries[i])
                if kind == "close":
                    acc[...] = states[i][0:VROWS]
                    top[...] = states[i][VROWS : VROWS + 1]

        n = jnp.int32(0)
        if has_own:
            todo[0] = OWN0 + 2 * chunk_z + chunk_core
            for t in range(4):
                todo[1 + t] = t

            def earlier(z, n):
                for r in range(4):
                    todo[n + 2 * r] = OWN0 + 8 * r + 2 * z
                    todo[n + 2 * r + 1] = OWN0 + 8 * r + 2 * z + 1
                return n + 8

            n = lax.fori_loop(0, chunk_z, earlier, jnp.int32(5))
            todo[n] = OWN0 + 2 * chunk_z
            n = n + chunk_core
            for r in range(1, 4):
                todo[n] = OWN0 + 8 * r + 2 * chunk_z
                todo[n + 1] = OWN0 + 8 * r + 2 * chunk_z + 1
                n = n + jnp.where(y >= r, 2, 0)
        if has_sib:
            for slot in range(NSIB):
                todo[n] = SIB0 + slot
                todo[n + 1] = SIB0 + 4 + slot
                n = n + jnp.where(plan[3 + slot, step] == 1, 2, 0)
        repeat = todo[1 if has_own else 0]
        for t in range(2 * SPAN):
            todo[n + t] = DUMMY
        kbuf[DUMMY] = kbuf[repeat]
        groups = lax.div(n + SPAN - 1, SPAN)

        def score(j, g):
            keys = jnp.concatenate([kbuf[todo[j * SPAN + t]] for t in range(SPAN)], axis=0)
            s_buf[g] = lax.dot_general(
                jnp.concatenate([keys, keys], axis=1),
                q_t[:, g * QW : (g + 1) * QW],
                (((1,), (0,)), ((), ())),
                preferred_element_type=jnp.float32,
            )

        def weigh(g, first=False):
            cols = slice(g * QW, (g + 1) * QW)
            s = s_buf[g]
            if first:
                key = lax.broadcasted_iota(jnp.int32, (TOK, QW), 0)
                token = lax.broadcasted_iota(jnp.int32, (TOK, QW), 1) % TOK
                s = jnp.concatenate([jnp.where(key <= token, s[0:TOK], HIDDEN), s[TOK:]], axis=0)
            peak = jnp.max(s, axis=0, keepdims=True)
            if not first:
                before = top[:, cols]
                peak = jnp.maximum(before, peak)
                a_buf[:, cols] = jnp.exp2(before - peak)
            top[:, cols] = peak
            p_buf[g] = jnp.exp2(s - peak).astype(jnp.bfloat16)

        def gather(j, g, first=False):
            cols = slice(g * QW, (g + 1) * QW)
            values_t = jnp.concatenate([vbuf[todo[j * SPAN + t]] for t in range(SPAN)], axis=1)
            part = lax.dot_general(
                values_t, p_buf[g], (((1,), (0,)), ((), ())), preferred_element_type=jnp.float32
            )
            acc[:, cols] = part if first else acc[:, cols] * a_buf[:, cols] + part

        last = HALVES - 1

        def turn(j, carry):
            for g in range(HALVES):
                if g == 0:
                    gather(j - 1, last)
                else:
                    gather(j, g - 1)
                weigh(g)
                if g < last:
                    score(j, g + 1)
                else:
                    score(j + 1, 0)
            return carry

        if has_own:
            score(0, 0)
            for g in range(HALVES):
                if g < last:
                    score(0, g + 1)
                else:
                    score(1, 0)
                if g:
                    gather(0, g - 1, first=True)
                weigh(g, first=True)
            acc[:, last * QW :] = jnp.zeros((VROWS, QW), jnp.float32)
            a_buf[:, last * QW :] = jnp.ones((1, QW), jnp.float32)
            lax.fori_loop(1, groups, turn, 0)
            gather(groups - 1, last)
        else:
            @pl.when(groups > 0)
            def _():
                for g in range(HALVES):
                    score(0, g)
                for g in range(HALVES):
                    weigh(g)
                    gather(0, g)

        def store(ref):
            if kind == "open":
                ref[0:VROWS] = acc[...]
                ref[VROWS:] = jnp.broadcast_to(top[...], (8, GROUP))
                return
            for h in range(KVH):
                cols = slice(h * HD, (h + 1) * HD)
                ref[:, cols] = (acc[0:HD, cols] / acc[HD : HD + 1, cols]).T.astype(jnp.bfloat16)

        for i in range(chunks):

            @pl.when(step == i)
            def _(i=i):
                store(outs[i])

    return kernel


def attend(kind, plan, queries, states, owns, sib):
    chunks = len(queries)

    def whole(a):
        return pl.BlockSpec(a.shape, lambda i, plan: (0,) * a.ndim, pipeline_mode=pl.Buffered(1))

    blocked = [*queries, *(states if kind == "close" else ())]
    raw = [*(owns if kind != "close" else ()), *((sib,) if kind != "open" else ())]
    if kind == "open":
        result = jax.ShapeDtypeStruct((VROWS + 8, GROUP), jnp.float32)
    else:
        result = jax.ShapeDtypeStruct((TOK, GROUP), jnp.bfloat16)
    return pl.pallas_call(
        make_kernel(kind, chunks),
        out_shape=(result,) * chunks,
        grid_spec=pltpu.PrefetchScalarGridSpec(
            num_scalar_prefetch=1,
            grid=(chunks,),
            in_specs=[whole(a) for a in blocked] + [pl.BlockSpec(memory_space=pl.ANY)] * len(raw),
            out_specs=[pl.BlockSpec(result.shape, lambda i, plan: (0, 0))] * chunks,
            scratch_shapes=[
                pltpu.VMEM((DUMMY + 1, TOK, HD), jnp.bfloat16),
                pltpu.VMEM((DUMMY + 1, VROWS, TOK), jnp.bfloat16),
                pltpu.VMEM((4, 8, 2 * PAST, HD), jnp.bfloat16),
                pltpu.SMEM((72,), jnp.int32),
                pltpu.VMEM((2 * HD, GROUP), jnp.bfloat16),
                pltpu.VMEM((HALVES, KB, QW), jnp.float32),
                pltpu.VMEM((HALVES, KB, QW), jnp.bfloat16),
                pltpu.VMEM((1, GROUP), jnp.float32),
                pltpu.VMEM((VROWS, GROUP), jnp.float32),
                pltpu.VMEM((1, GROUP), jnp.float32),
                pltpu.SemaphoreType.DMA((16,)),
            ],
        ),
        compiler_params=pltpu.CompilerParams(vmem_limit_bytes=32 * 2**20),
    )(plan, *blocked, *raw)


def shifted(value, axis, by):
    n = lax.axis_size(axis)
    return lax.ppermute(value, axis, [(k, (k + by) % n) for k in range(n)])


def exchanged(value, step):
    return lax.ppermute(value, (Z, CORE), [(k, k ^ step) for k in range(8)])


def after(value, *others):
    return lax.optimization_barrier((value, *others))[0]


def packing(key_ref, value_ref, past_key_ref, past_value_ref, out_ref):
    for h in range(KVH):
        cols = slice(h * HD, (h + 1) * HD)
        out_ref[h, 0:TOK] = key_ref[0, :, cols]
        out_ref[h, TOK : TOK + HD] = value_ref[0, :, cols].T
        out_ref[h, TOK + HD : TOK + HD + PAST] = past_key_ref[:, cols]
        out_ref[h, TOK + HD + PAST :] = past_value_ref[:, cols]


def packed(*arrays):
    shape = jax.ShapeDtypeStruct((KVH, TOK + HD + 2 * PAST, HD), jnp.bfloat16)
    return pl.pallas_call(packing, out_shape=shape, name="packing")(*arrays)


def attention(query, key_new, value_new, hist_key, hist_value, sib_source, sib_block, sib_mask):
    z, y, core = lax.axis_index(Z), lax.axis_index(Y), lax.axis_index(CORE)
    me = z * 2 + core
    reader = lax.axis_index("branch")

    send = packed(key_new, value_new, hist_key, hist_value)
    own = lax.all_to_all(send, (Z, CORE), split_axis=0, concat_axis=0, tiled=True)
    up, down = shifted(own, Y, 1), shifted(own, Y, -1)
    onward = shifted(up[:4], Y, 1), shifted(down[4:], Y, -1)
    over = jnp.concatenate(onward, axis=0)
    owns = (own, up, over, down)

    cols = after(query[0], own)
    queries = {}
    for s in QORDER:
        piece = lax.dynamic_slice_in_dim(cols, (me ^ s) * GROUP, GROUP, 1)
        queries[s] = exchanged(piece, s) if s else piece

    start = TOK * (y // 2)
    mine = jnp.concatenate(
        [
            lax.dynamic_slice(o.reshape(4, 2, -1, HD), (0, y % 2, start, 0), (4, 1, TOK, HD)).reshape(4, TOK, HD)
            for o in owns
        ]
    )
    my_source = lax.dynamic_index_in_dim(sib_source, reader, 0, keepdims=False)
    my_mask = lax.dynamic_index_in_dim(sib_mask, reader, 0, keepdims=False)
    from_me = sib_source == reader
    sender_rank = jnp.cumsum(from_me.astype(jnp.int32), axis=1) - 1
    slot_hit = from_me[:, :, None] & (
        sender_rank[:, :, None] == jnp.arange(SRCMAX, dtype=jnp.int32)[None, None, :]
    )
    send_table = jnp.sum(jnp.where(slot_hit, sib_block[:, :, None], 0), axis=1)
    place = ((y - send_table) % 4) * 4 + send_table // 4
    got = lax.all_to_all(mine[place], "branch", split_axis=0, concat_axis=0, tiled=True)
    slots = jnp.arange(NSIB, dtype=jnp.int32)
    same = (my_source[None, :] == my_source[:, None]) & (slots[None, :] < slots[:, None])
    rank = jnp.sum(same.astype(jnp.int32), axis=1)
    listed = got.reshape(-1, HD, HD)[my_source * SRCMAX + rank]
    sib = jnp.stack([listed, shifted(listed, Y, 1), shifted(listed, Y, 2), shifted(listed, Y, -1)])

    def plan_of(steps):
        chunks = jnp.stack([me ^ s for s in steps])
        visible = my_mask[(chunks // 2) * 4 + y]
        rows = [(chunks // 2)[None], (chunks % 2)[None], jnp.broadcast_to(y, (1, len(steps))), visible.T]
        return jnp.concatenate(rows, axis=0).astype(jnp.int32)

    parts, states, previous = {}, {}, None
    for kind, steps in CALLS:
        asked = [queries[s] for s in steps]
        if previous is not None:
            asked[0] = after(asked[0], previous)
        results = attend(kind, plan_of(steps), asked, [states.get(s) for s in steps], owns, sib)
        previous = results[0]
        for s, result in zip(steps, results):
            if kind == "open":
                states[s] = result
            else:
                parts[s] = exchanged(result, s) if s else result
    out = jnp.zeros((TOK, KVH * GROUP), jnp.bfloat16)
    for s in range(8):
        out = lax.dynamic_update_slice_in_dim(out, parts[s], (me ^ s) * GROUP, 1)
    return out[None]


QORDER = (2, 3, 4, 5, 6, 7, 1, 0)
CALLS = (("open", (2, 3)), ("full", (4, 5)), ("close", (2, 3)), ("full", (6, 7)), ("full", (1, 0)))


def solution(mesh):
    split = Mesh(mesh.devices.reshape(mesh.shape["branch"], 4, 4, 2), ("branch", Z, Y, CORE))
    seq = (Z, Y, CORE)
    placed = (
        P("branch", seq, None),
        P("branch", seq, None),
        P("branch", seq, None),
        P(seq, None),
        P(seq, None),
        P(),
        P(),
        P(),
    )
    return jax.shard_map(
        attention, mesh=split, in_specs=placed, out_specs=P("branch", seq, None), check_vma=False
    )
```

```python
import math

import jax
import jax.numpy as jnp
from jax import lax
from jax.experimental import pallas as pl
from jax.experimental.pallas import tpu as pltpu
from jax.sharding import Mesh
from jax.sharding import PartitionSpec as P


KVH = 8
HD = 128
NSIB = 4
SRCMAX = 2
TOK = 128
PAST = 16
GROUP = 1024
Z, Y, CORE = "seq_0", "seq_1", "seq_2"
EXP2_SCALE = math.log2(math.e) / math.sqrt(HD)
HIDDEN = -1e30
OWN0, SIB0, DUMMY = 4, 36, 44
VROWS = HD + 16
SPAN = 8
QW = 512
HALVES = GROUP // QW
KB = SPAN * TOK


def make_kernel(kind, chunks):
    has_own, has_sib = kind != "close", kind != "open"

    def kernel(plan, *refs):
        refs = list(refs)

        def take(count):
            taken = refs[:count]
            del refs[:count]
            return taken

        queries = take(chunks)
        states = take(chunks) if kind == "close" else []
        owns = take(4) if has_own else []
        sibs = take(1) if has_sib else []
        outs = take(chunks)
        kbuf, vbuf, past, todo, q_t, s_buf, p_buf, a_buf, acc, top, sem = refs
        step = pl.program_id(0)
        chunk_z, chunk_core, y = plan[0, step], plan[1, step], plan[2, step]

        @pl.when(step == 0)
        def _():
            pairs = []
            for r, own in enumerate(owns):
                here = pl.ds(OWN0 + 8 * r, 8)
                pairs.append((own.at[:, pl.ds(0, TOK)], kbuf.at[here]))
                pairs.append((own.at[:, pl.ds(TOK, HD)], vbuf.at[here, pl.ds(0, HD)]))
                pairs.append((own.at[:, pl.ds(TOK + HD, 2 * PAST)], past.at[r]))
            for slot in range(NSIB if has_sib else 0):
                source = sibs[0].at[plan[3 + NSIB + slot, 0]]
                here = pl.ds(SIB0 + 2 * slot, 2)
                pairs.append((source.at[:, pl.ds(0, TOK)], kbuf.at[here]))
                pairs.append((source.at[:, pl.ds(TOK, HD)], vbuf.at[here, pl.ds(0, HD)]))
            copies = [pltpu.make_async_copy(a, b, sem.at[i]) for i, (a, b) in enumerate(pairs)]
            for copy in copies:
                copy.start()
            row = lax.broadcasted_iota(jnp.int32, (VROWS - HD, TOK), 0)
            ones = jnp.where(row == 0, 1.0, 0.0).astype(jnp.bfloat16)
            for t in range(DUMMY):
                vbuf[t, HD:VROWS, :] = ones
            vbuf[DUMMY] = jnp.zeros((VROWS, TOK), jnp.bfloat16)
            for copy in copies:
                copy.wait()
            for r in range(len(owns)):
                kbuf[r] = past[r, :, 0:PAST].reshape(TOK, HD)
                vbuf[r, 0:HD] = past[r, :, PAST : 2 * PAST].reshape(TOK, HD).T

        def load(ref):
            for h in range(KVH):
                cols = slice(h * HD, (h + 1) * HD)
                scaled = ref[:, cols].T.astype(jnp.float32) * EXP2_SCALE
                upper = scaled.astype(jnp.bfloat16)
                q_t[0:HD, cols] = upper
                q_t[HD : 2 * HD, cols] = (scaled - upper.astype(jnp.float32)).astype(jnp.bfloat16)

        for i in range(chunks):

            @pl.when(step == i)
            def _(i=i):
                load(queries[i])
                if kind == "close":
                    acc[...] = states[i][0:VROWS]
                    top[...] = states[i][VROWS : VROWS + 1]

        n = jnp.int32(0)
        if has_own:
            todo[0] = OWN0 + 2 * chunk_z + chunk_core
            for t in range(4):
                todo[1 + t] = t

            def earlier(z, n):
                for r in range(4):
                    todo[n + 2 * r] = OWN0 + 8 * r + 2 * z
                    todo[n + 2 * r + 1] = OWN0 + 8 * r + 2 * z + 1
                return n + 8

            n = lax.fori_loop(0, chunk_z, earlier, jnp.int32(5))
            todo[n] = OWN0 + 2 * chunk_z
            n = n + chunk_core
            for r in range(1, 4):
                todo[n] = OWN0 + 8 * r + 2 * chunk_z
                todo[n + 1] = OWN0 + 8 * r + 2 * chunk_z + 1
                n = n + jnp.where(y >= r, 2, 0)
        if has_sib:
            for slot in range(NSIB):
                todo[n] = SIB0 + 2 * slot
                todo[n + 1] = SIB0 + 2 * slot + 1
                n = n + jnp.where(plan[3 + slot, step] == 1, 2, 0)
        repeat = todo[1 if has_own else 0]
        for t in range(2 * SPAN):
            todo[n + t] = DUMMY
        kbuf[DUMMY] = kbuf[repeat]
        groups = lax.div(n + SPAN - 1, SPAN)

        def score(j, g):
            keys = jnp.concatenate([kbuf[todo[j * SPAN + t]] for t in range(SPAN)], axis=0)
            s_buf[g] = lax.dot_general(
                jnp.concatenate([keys, keys], axis=1),
                q_t[:, g * QW : (g + 1) * QW],
                (((1,), (0,)), ((), ())),
                preferred_element_type=jnp.float32,
            )

        def weigh(g, first=False):
            cols = slice(g * QW, (g + 1) * QW)
            s = s_buf[g]
            if first:
                key = lax.broadcasted_iota(jnp.int32, (TOK, QW), 0)
                token = lax.broadcasted_iota(jnp.int32, (TOK, QW), 1) % TOK
                s = jnp.concatenate([jnp.where(key <= token, s[0:TOK], HIDDEN), s[TOK:]], axis=0)
            peak = jnp.max(s, axis=0, keepdims=True)
            if not first:
                before = top[:, cols]
                peak = jnp.maximum(before, peak)
                a_buf[:, cols] = jnp.exp2(before - peak)
            top[:, cols] = peak
            p_buf[g] = jnp.exp2(s - peak).astype(jnp.bfloat16)

        def gather(j, g, first=False):
            cols = slice(g * QW, (g + 1) * QW)
            values_t = jnp.concatenate([vbuf[todo[j * SPAN + t]] for t in range(SPAN)], axis=1)
            part = lax.dot_general(
                values_t, p_buf[g], (((1,), (0,)), ((), ())), preferred_element_type=jnp.float32
            )
            acc[:, cols] = part if first else acc[:, cols] * a_buf[:, cols] + part

        last = HALVES - 1

        def turn(j, carry):
            for g in range(HALVES):
                if g == 0:
                    gather(j - 1, last)
                else:
                    gather(j, g - 1)
                weigh(g)
                if g < last:
                    score(j, g + 1)
                else:
                    score(j + 1, 0)
            return carry

        if has_own:
            score(0, 0)
            for g in range(HALVES):
                if g < last:
                    score(0, g + 1)
                else:
                    score(1, 0)
                if g:
                    gather(0, g - 1, first=True)
                weigh(g, first=True)
            acc[:, last * QW :] = jnp.zeros((VROWS, QW), jnp.float32)
            a_buf[:, last * QW :] = jnp.ones((1, QW), jnp.float32)
            lax.fori_loop(1, groups, turn, 0)
            gather(groups - 1, last)
        else:
            @pl.when(groups > 0)
            def _():
                for g in range(HALVES):
                    score(0, g)
                for g in range(HALVES):
                    weigh(g)
                    gather(0, g)

        def store(ref):
            if kind == "open":
                ref[0:VROWS] = acc[...]
                ref[VROWS:] = jnp.broadcast_to(top[...], (8, GROUP))
                return
            for h in range(KVH):
                cols = slice(h * HD, (h + 1) * HD)
                ref[:, cols] = (acc[0:HD, cols] / acc[HD : HD + 1, cols]).T.astype(jnp.bfloat16)

        for i in range(chunks):

            @pl.when(step == i)
            def _(i=i):
                store(outs[i])

    return kernel


def attend(kind, plan, queries, states, owns, sib):
    chunks = len(queries)

    def whole(a):
        return pl.BlockSpec(a.shape, lambda i, plan: (0,) * a.ndim, pipeline_mode=pl.Buffered(1))

    blocked = [*queries, *(states if kind == "close" else ())]
    raw = [*(owns if kind != "close" else ()), *((sib,) if kind != "open" else ())]
    if kind == "open":
        result = jax.ShapeDtypeStruct((VROWS + 8, GROUP), jnp.float32)
    else:
        result = jax.ShapeDtypeStruct((TOK, GROUP), jnp.bfloat16)
    return pl.pallas_call(
        make_kernel(kind, chunks),
        out_shape=(result,) * chunks,
        grid_spec=pltpu.PrefetchScalarGridSpec(
            num_scalar_prefetch=1,
            grid=(chunks,),
            in_specs=[whole(a) for a in blocked] + [pl.BlockSpec(memory_space=pl.ANY)] * len(raw),
            out_specs=[pl.BlockSpec(result.shape, lambda i, plan: (0, 0))] * chunks,
            scratch_shapes=[
                pltpu.VMEM((DUMMY + 1, TOK, HD), jnp.bfloat16),
                pltpu.VMEM((DUMMY + 1, VROWS, TOK), jnp.bfloat16),
                pltpu.VMEM((4, 8, 2 * PAST, HD), jnp.bfloat16),
                pltpu.SMEM((72,), jnp.int32),
                pltpu.VMEM((2 * HD, GROUP), jnp.bfloat16),
                pltpu.VMEM((HALVES, KB, QW), jnp.float32),
                pltpu.VMEM((HALVES, KB, QW), jnp.bfloat16),
                pltpu.VMEM((1, GROUP), jnp.float32),
                pltpu.VMEM((VROWS, GROUP), jnp.float32),
                pltpu.VMEM((1, GROUP), jnp.float32),
                pltpu.SemaphoreType.DMA((20,)),
            ],
        ),
        compiler_params=pltpu.CompilerParams(vmem_limit_bytes=32 * 2**20),
    )(plan, *blocked, *raw)


def shifted(value, axis, by):
    n = lax.axis_size(axis)
    return lax.ppermute(value, axis, [(k, (k + by) % n) for k in range(n)])


def exchanged(value, step):
    return lax.ppermute(value, (Z, CORE), [(k, k ^ step) for k in range(8)])


def after(value, *others):
    return lax.optimization_barrier((value, *others))[0]


def packing(key_ref, value_ref, past_key_ref, past_value_ref, out_ref):
    for h in range(KVH):
        cols = slice(h * HD, (h + 1) * HD)
        out_ref[h, 0:TOK] = key_ref[0, :, cols]
        out_ref[h, TOK : TOK + HD] = value_ref[0, :, cols].T
        out_ref[h, TOK + HD : TOK + HD + PAST] = past_key_ref[:, cols]
        out_ref[h, TOK + HD + PAST :] = past_value_ref[:, cols]


def packed(*arrays):
    shape = jax.ShapeDtypeStruct((KVH, TOK + HD + 2 * PAST, HD), jnp.bfloat16)
    return pl.pallas_call(packing, out_shape=shape, name="packing")(*arrays)


def picking(where, own0, own1, own2, own3, out_ref, sem):
    count = out_ref.shape[0]

    def copy(own, e):
        pair = own.at[pl.ds(2 * where[count + e], 2), pl.ds(0, TOK + HD)]
        return pltpu.make_async_copy(pair, out_ref.at[e], sem.at[e])

    for e in range(count):
        for r, own in enumerate((own0, own1, own2, own3)):

            @pl.when(where[e] == r)
            def _(own=own, e=e):
                copy(own, e).start()

    for e in range(count):
        copy(own0, e).wait()


def picked(where, owns):
    entries = where.shape[0] // 2
    raw = pl.BlockSpec(memory_space=pl.ANY)
    return pl.pallas_call(
        picking,
        out_shape=jax.ShapeDtypeStruct((entries, 2, TOK + HD, HD), jnp.bfloat16),
        grid_spec=pltpu.PrefetchScalarGridSpec(
            num_scalar_prefetch=1,
            grid=(1,),
            in_specs=[raw] * 4,
            out_specs=raw,
            scratch_shapes=[pltpu.SemaphoreType.DMA((entries,))],
        ),
        name="picking",
    )(where, *owns)


def attention(query, key_new, value_new, hist_key, hist_value, sib_source, sib_block, sib_mask):
    z, y, core = lax.axis_index(Z), lax.axis_index(Y), lax.axis_index(CORE)
    me = z * 2 + core
    reader = lax.axis_index("branch")

    send = packed(key_new, value_new, hist_key, hist_value)
    own = lax.all_to_all(send, (Z, CORE), split_axis=0, concat_axis=0, tiled=True)
    up, down = shifted(own, Y, 1), shifted(own, Y, -1)
    onward = shifted(up[:4], Y, 1), shifted(down[4:], Y, -1)
    over = jnp.concatenate(onward, axis=0)
    owns = (own, up, over, down)

    cols = after(query[0], own)
    queries = {}
    for s in QORDER:
        piece = lax.dynamic_slice_in_dim(cols, (me ^ s) * GROUP, GROUP, 1)
        queries[s] = exchanged(piece, s) if s else piece

    my_source = lax.dynamic_index_in_dim(sib_source, reader, 0, keepdims=False)
    my_mask = lax.dynamic_index_in_dim(sib_mask, reader, 0, keepdims=False)
    from_me = sib_source == reader
    sender_rank = jnp.cumsum(from_me.astype(jnp.int32), axis=1) - 1
    slot_hit = from_me[:, :, None] & (
        sender_rank[:, :, None] == jnp.arange(SRCMAX, dtype=jnp.int32)[None, None, :]
    )
    send_table = jnp.sum(jnp.where(slot_hit, sib_block[:, :, None], 0), axis=1).reshape(-1)
    where = jnp.concatenate([(y - send_table) % 4, send_table // 4]).astype(jnp.int32)
    sent = picked(where, owns)
    sib = lax.all_to_all(sent, "branch", split_axis=0, concat_axis=0, tiled=True)
    slots = jnp.arange(NSIB, dtype=jnp.int32)
    same = (my_source[None, :] == my_source[:, None]) & (slots[None, :] < slots[:, None])
    rank = jnp.sum(same.astype(jnp.int32), axis=1)
    flat = (my_source * SRCMAX + rank).astype(jnp.int32)

    def plan_of(steps):
        chunks = jnp.stack([me ^ s for s in steps])
        visible = my_mask[(chunks // 2) * 4 + y]
        rows = [(chunks // 2)[None], (chunks % 2)[None], jnp.broadcast_to(y, (1, len(steps))), visible.T]
        rows.append(jnp.broadcast_to(flat[:, None], (NSIB, len(steps))))
        return jnp.concatenate(rows, axis=0).astype(jnp.int32)

    parts, states, previous = {}, {}, None
    for kind, steps in CALLS:
        asked = [queries[s] for s in steps]
        if previous is not None:
            asked[0] = after(asked[0], previous)
        results = attend(kind, plan_of(steps), asked, [states.get(s) for s in steps], owns, sib)
        previous = results[0]
        for s, result in zip(steps, results):
            if kind == "open":
                states[s] = result
            else:
                parts[s] = exchanged(result, s) if s else result
    out = jnp.zeros((TOK, KVH * GROUP), jnp.bfloat16)
    for s in range(8):
        out = lax.dynamic_update_slice_in_dim(out, parts[s], (me ^ s) * GROUP, 1)
    return out[None]


QORDER = (2, 4, 3, 5, 6, 7, 1, 0)
CALLS = (("open", (2, 4)), ("full", (3, 5)), ("close", (2, 4)), ("full", (6, 0)), ("full", (7, 1)))


def solution(mesh):
    split = Mesh(mesh.devices.reshape(mesh.shape["branch"], 4, 4, 2), ("branch", Z, Y, CORE))
    seq = (Z, Y, CORE)
    placed = (
        P("branch", seq, None),
        P("branch", seq, None),
        P("branch", seq, None),
        P(seq, None),
        P(seq, None),
        P(),
        P(),
        P(),
    )
    return jax.shard_map(
        attention, mesh=split, in_specs=placed, out_specs=P("branch", seq, None), check_vma=False
    )
```

```python
import math

import jax
import jax.numpy as jnp
from jax import lax
from jax.experimental import pallas as pl
from jax.experimental.pallas import tpu as pltpu
from jax.sharding import Mesh
from jax.sharding import PartitionSpec as P


KVH = 8
HD = 128
NSIB = 4
SRCMAX = 2
TOK = 128
PAST = 16
GROUP = 1024
Z, Y, CORE = "seq_0", "seq_1", "seq_2"
EXP2_SCALE = math.log2(math.e) / math.sqrt(HD)
HIDDEN = -1e30
OWN0, SIB0, DUMMY = 4, 36, 44
VROWS = HD + 16
SPAN = 4
QW = 512
HALVES = GROUP // QW
KB = SPAN * TOK


def in_hbm(array):
    return pltpu.with_memory_space_constraint(array, pltpu.HBM)


def make_kernel(kind, chunks):
    has_own, has_sib = kind != "close", kind != "open"

    def kernel(plan, *refs):
        refs = list(refs)

        def take(count):
            taken = refs[:count]
            del refs[:count]
            return taken

        queries = take(chunks)
        states = take(chunks) if kind == "close" else []
        owns = take(4) if kind == "open" else []
        sibs = take(1) if kind == "close" else []
        kbuf, vbuf = take(2) if kind != "open" else (None, None)
        outs = take(chunks)
        if kind != "full":
            kbuf, vbuf = take(2)
        todo, q_t, s_buf, p_buf, a_buf, acc, top = take(7)
        past = take(1)[0] if kind == "open" else None
        sem = take(1)[0] if kind != "full" else None
        step = pl.program_id(0)
        chunk_z, chunk_core, y = plan[0, step], plan[1, step], plan[2, step]

        def fill():
            pairs = []
            for r, own in enumerate(owns):
                here = pl.ds(OWN0 + 8 * r, 8)
                pairs.append((own.at[:, pl.ds(0, TOK)], kbuf.at[here]))
                pairs.append((own.at[:, pl.ds(TOK, HD)], vbuf.at[here, pl.ds(0, HD)]))
                pairs.append((own.at[:, pl.ds(TOK + HD, 2 * PAST)], past.at[r]))
            for slot in range(NSIB if sibs else 0):
                source = sibs[0].at[plan[3 + NSIB + slot, 0]]
                here = pl.ds(SIB0 + 2 * slot, 2)
                pairs.append((source.at[:, pl.ds(0, TOK)], kbuf.at[here]))
                pairs.append((source.at[:, pl.ds(TOK, HD)], vbuf.at[here, pl.ds(0, HD)]))
            copies = [pltpu.make_async_copy(a, b, sem.at[i]) for i, (a, b) in enumerate(pairs)]
            for copy in copies:
                copy.start()
            if owns:
                row = lax.broadcasted_iota(jnp.int32, (VROWS - HD, TOK), 0)
                ones = jnp.where(row == 0, 1.0, 0.0).astype(jnp.bfloat16)
                for t in range(DUMMY):
                    vbuf[t, HD:VROWS, :] = ones
                vbuf[DUMMY] = jnp.zeros((VROWS, TOK), jnp.bfloat16)
            for copy in copies:
                copy.wait()
            for r in range(len(owns)):
                kbuf[r] = past[r, :, 0:PAST].reshape(TOK, HD)
                vbuf[r, 0:HD] = past[r, :, PAST : 2 * PAST].reshape(TOK, HD).T
            if owns:
                kbuf[DUMMY] = kbuf[0]

        if kind != "full":
            pl.when(step == 0)(fill)

        def load(ref):
            for h in range(KVH):
                cols = slice(h * HD, (h + 1) * HD)
                scaled = ref[:, cols].T.astype(jnp.float32) * EXP2_SCALE
                upper = scaled.astype(jnp.bfloat16)
                q_t[0:HD, cols] = upper
                q_t[HD : 2 * HD, cols] = (scaled - upper.astype(jnp.float32)).astype(jnp.bfloat16)

        for i in range(chunks):

            @pl.when(step == i)
            def _(i=i):
                load(queries[i])
                if kind == "close":
                    acc[...] = states[i][0:VROWS]
                    top[...] = states[i][VROWS : VROWS + 1]

        n = jnp.int32(0)
        if has_own:
            todo[0] = OWN0 + 2 * chunk_z + chunk_core
            for t in range(4):
                todo[1 + t] = t

            def earlier(z, n):
                for r in range(4):
                    todo[n + 2 * r] = OWN0 + 8 * r + 2 * z
                    todo[n + 2 * r + 1] = OWN0 + 8 * r + 2 * z + 1
                return n + 8

            n = lax.fori_loop(0, chunk_z, earlier, jnp.int32(5))
            todo[n] = OWN0 + 2 * chunk_z
            n = n + chunk_core
            for r in range(1, 4):
                todo[n] = OWN0 + 8 * r + 2 * chunk_z
                todo[n + 1] = OWN0 + 8 * r + 2 * chunk_z + 1
                n = n + jnp.where(y >= r, 2, 0)
        if has_sib:
            for slot in range(NSIB):
                todo[n] = SIB0 + 2 * slot
                todo[n + 1] = SIB0 + 2 * slot + 1
                n = n + jnp.where(plan[3 + slot, step] == 1, 2, 0)
        for t in range(2 * SPAN):
            todo[n + t] = DUMMY
        groups = lax.div(n + SPAN - 1, SPAN)

        def score(j, g):
            keys = jnp.concatenate([kbuf[todo[j * SPAN + t]] for t in range(SPAN)], axis=0)
            s_buf[g] = lax.dot_general(
                jnp.concatenate([keys, keys], axis=1),
                q_t[:, g * QW : (g + 1) * QW],
                (((1,), (0,)), ((), ())),
                preferred_element_type=jnp.float32,
            )

        def weigh(g, first=False):
            cols = slice(g * QW, (g + 1) * QW)
            s = s_buf[g]
            if first:
                key = lax.broadcasted_iota(jnp.int32, (TOK, QW), 0)
                token = lax.broadcasted_iota(jnp.int32, (TOK, QW), 1) % TOK
                s = jnp.concatenate([jnp.where(key <= token, s[0:TOK], HIDDEN), s[TOK:]], axis=0)
            peak = jnp.max(s, axis=0, keepdims=True)
            if not first:
                before = top[:, cols]
                peak = jnp.maximum(before, peak)
                a_buf[:, cols] = jnp.exp2(before - peak)
            top[:, cols] = peak
            p_buf[g] = jnp.exp2(s - peak).astype(jnp.bfloat16)

        def gather(j, g, first=False):
            cols = slice(g * QW, (g + 1) * QW)
            values_t = jnp.concatenate([vbuf[todo[j * SPAN + t]] for t in range(SPAN)], axis=1)
            part = lax.dot_general(
                values_t, p_buf[g], (((1,), (0,)), ((), ())), preferred_element_type=jnp.float32
            )
            acc[:, cols] = part if first else acc[:, cols] * a_buf[:, cols] + part

        last = HALVES - 1

        def turn(j, carry):
            for g in range(HALVES):
                if g == 0:
                    gather(j - 1, last)
                else:
                    gather(j, g - 1)
                weigh(g)
                if g < last:
                    score(j, g + 1)
                else:
                    score(j + 1, 0)
            return carry

        if has_own:
            score(0, 0)
            for g in range(HALVES):
                if g < last:
                    score(0, g + 1)
                else:
                    score(1, 0)
                if g:
                    gather(0, g - 1, first=True)
                weigh(g, first=True)
            acc[:, last * QW :] = jnp.zeros((VROWS, QW), jnp.float32)
            a_buf[:, last * QW :] = jnp.ones((1, QW), jnp.float32)
            lax.fori_loop(1, groups, turn, 0)
            gather(groups - 1, last)
        else:
            def listed(j, carry):
                for g in range(HALVES):
                    score(j, g)
                for g in range(HALVES):
                    weigh(g)
                    gather(j, g)
                return carry

            lax.fori_loop(0, groups, listed, 0)

        def store(ref):
            if kind == "open":
                ref[0:VROWS] = acc[...]
                ref[VROWS:] = jnp.broadcast_to(top[...], (8, GROUP))
                return
            for h in range(KVH):
                cols = slice(h * HD, (h + 1) * HD)
                ref[:, cols] = (acc[0:HD, cols] / acc[HD : HD + 1, cols]).T.astype(jnp.bfloat16)

        for i in range(chunks):

            @pl.when(step == i)
            def _(i=i):
                store(outs[i])

    return kernel


def attend(kind, plan, queries, states, source, buffers):
    chunks = len(queries)

    def whole(a):
        return pl.BlockSpec(a.shape, lambda i, plan: (0,) * a.ndim, pipeline_mode=pl.Buffered(1))

    blocked = [*queries, *(states if kind == "close" else ())]
    raw = list(source) if kind != "full" else []
    kept = list(buffers) if kind != "open" else []
    if kind == "open":
        result = jax.ShapeDtypeStruct((VROWS + 8, GROUP), jnp.float32)
    else:
        result = jax.ShapeDtypeStruct((TOK, GROUP), jnp.bfloat16)
    tile_shapes = [(DUMMY + 1, TOK, HD), (DUMMY + 1, VROWS, TOK)]
    tiles = [jax.ShapeDtypeStruct(shape, jnp.bfloat16) for shape in tile_shapes] if kind != "full" else []
    resident = pl.BlockSpec(memory_space=pltpu.VMEM)
    scratch = [
        pltpu.SMEM((72,), jnp.int32),
        pltpu.VMEM((2 * HD, GROUP), jnp.bfloat16),
        pltpu.VMEM((HALVES, KB, QW), jnp.float32),
        pltpu.VMEM((HALVES, KB, QW), jnp.bfloat16),
        pltpu.VMEM((1, GROUP), jnp.float32),
        pltpu.VMEM((VROWS, GROUP), jnp.float32),
        pltpu.VMEM((1, GROUP), jnp.float32),
    ]
    if kind == "open":
        scratch.append(pltpu.VMEM((4, 8, 2 * PAST, HD), jnp.bfloat16))
    if kind != "full":
        scratch.append(pltpu.SemaphoreType.DMA((16,)))
    first_kept = 1 + len(blocked) + len(raw)
    aliases = {first_kept: chunks, first_kept + 1: chunks + 1} if kind == "close" else {}
    return pl.pallas_call(
        make_kernel(kind, chunks),
        out_shape=(result,) * chunks + tuple(tiles),
        grid_spec=pltpu.PrefetchScalarGridSpec(
            num_scalar_prefetch=1,
            grid=(chunks,),
            in_specs=[whole(a) for a in blocked]
            + [pl.BlockSpec(memory_space=pltpu.HBM)] * len(raw)
            + [resident] * len(kept),
            out_specs=[pl.BlockSpec(result.shape, lambda i, plan: (0, 0))] * chunks + [resident] * len(tiles),
            scratch_shapes=scratch,
        ),
        input_output_aliases=aliases,
        compiler_params=pltpu.CompilerParams(vmem_limit_bytes=24 * 2**20),
    )(plan, *[in_hbm(a) for a in blocked], *[in_hbm(a) for a in raw], *kept)


def shifted(value, axis, by):
    n = lax.axis_size(axis)
    return lax.ppermute(value, axis, [(k, (k + by) % n) for k in range(n)])


def exchanged(value, step):
    return lax.ppermute(value, (Z, CORE), [(k, k ^ step) for k in range(8)])


def after(value, *others):
    return lax.optimization_barrier((value, *others))[0]


def packing(key_ref, value_ref, past_key_ref, past_value_ref, out_ref):
    for h in range(KVH):
        cols = slice(h * HD, (h + 1) * HD)
        out_ref[h, 0:TOK] = key_ref[0, :, cols]
        out_ref[h, TOK : TOK + HD] = value_ref[0, :, cols].T
        out_ref[h, TOK + HD : TOK + HD + PAST] = past_key_ref[:, cols]
        out_ref[h, TOK + HD + PAST :] = past_value_ref[:, cols]


def packed(*arrays):
    shape = jax.ShapeDtypeStruct((KVH, TOK + HD + 2 * PAST, HD), jnp.bfloat16)
    return pl.pallas_call(packing, out_shape=shape, name="packing")(*arrays)


def picking(where, own0, own1, own2, own3, out_ref):
    count = out_ref.shape[0]
    for e in range(count):
        for r, own in enumerate((own0, own1, own2, own3)):

            @pl.when(where[e] == r)
            def _(own=own, e=e):
                out_ref[e] = own[pl.ds(2 * where[count + e], 2), 0 : TOK + HD]


def picked(where, owns):
    entries = where.shape[0] // 2
    shape = (entries, 2, TOK + HD, HD)
    whole = pl.BlockSpec(owns[0].shape, lambda i, where: (0, 0, 0), pipeline_mode=pl.Buffered(1))
    return pl.pallas_call(
        picking,
        out_shape=jax.ShapeDtypeStruct(shape, jnp.bfloat16),
        grid_spec=pltpu.PrefetchScalarGridSpec(
            num_scalar_prefetch=1,
            grid=(1,),
            in_specs=[whole] * 4,
            out_specs=pl.BlockSpec(shape, lambda i, where: (0, 0, 0, 0), pipeline_mode=pl.Buffered(1)),
        ),
        compiler_params=pltpu.CompilerParams(vmem_limit_bytes=16 * 2**20),
        name="picking",
    )(where, *[in_hbm(own) for own in owns])


def attention(query, key_new, value_new, hist_key, hist_value, sib_source, sib_block, sib_mask):
    z, y, core = lax.axis_index(Z), lax.axis_index(Y), lax.axis_index(CORE)
    me = z * 2 + core
    reader = lax.axis_index("branch")

    send = packed(key_new, value_new, hist_key, hist_value)
    own = lax.all_to_all(send, (Z, CORE), split_axis=0, concat_axis=0, tiled=True)
    up, down = shifted(own, Y, 1), shifted(own, Y, -1)
    onward = shifted(up[:4], Y, 1), shifted(down[4:], Y, -1)
    over = jnp.concatenate(onward, axis=0)
    owns = (own, up, over, down)

    cols = after(query[0], own)
    queries = {}
    for s in QORDER:
        piece = lax.dynamic_slice_in_dim(cols, (me ^ s) * GROUP, GROUP, 1)
        queries[s] = exchanged(piece, s) if s else piece

    my_source = lax.dynamic_index_in_dim(sib_source, reader, 0, keepdims=False)
    my_mask = lax.dynamic_index_in_dim(sib_mask, reader, 0, keepdims=False)
    from_me = sib_source == reader
    sender_rank = jnp.cumsum(from_me.astype(jnp.int32), axis=1) - 1
    slot_hit = from_me[:, :, None] & (
        sender_rank[:, :, None] == jnp.arange(SRCMAX, dtype=jnp.int32)[None, None, :]
    )
    send_table = jnp.sum(jnp.where(slot_hit, sib_block[:, :, None], 0), axis=1).reshape(-1)
    where = jnp.concatenate([(y - send_table) % 4, send_table // 4]).astype(jnp.int32)
    sent = picked(where, owns)
    sib = lax.all_to_all(sent, "branch", split_axis=0, concat_axis=0, tiled=True)
    slots = jnp.arange(NSIB, dtype=jnp.int32)
    same = (my_source[None, :] == my_source[:, None]) & (slots[None, :] < slots[:, None])
    rank = jnp.sum(same.astype(jnp.int32), axis=1)
    flat = (my_source * SRCMAX + rank).astype(jnp.int32)

    def plan_of(steps):
        chunks = jnp.stack([me ^ s for s in steps])
        visible = my_mask[(chunks // 2) * 4 + y]
        rows = [(chunks // 2)[None], (chunks % 2)[None], jnp.broadcast_to(y, (1, len(steps))), visible.T]
        rows.append(jnp.broadcast_to(flat[:, None], (NSIB, len(steps))))
        return jnp.concatenate(rows, axis=0).astype(jnp.int32)

    parts, states, previous, buffers = {}, {}, None, ()
    for kind, steps in CALLS:
        asked = [queries[s] for s in steps]
        if previous is not None:
            asked[0] = after(asked[0], previous)
        source = owns if kind == "open" else (sib,)
        results = attend(kind, plan_of(steps), asked, [states.get(s) for s in steps], source, buffers)
        if kind != "full":
            buffers = results[len(steps) :]
        previous = results[0]
        for s, result in zip(steps, results):
            if kind == "open":
                states[s] = result
            else:
                parts[s] = exchanged(result, s) if s else result
    out = jnp.zeros((TOK, KVH * GROUP), jnp.bfloat16)
    for s in range(8):
        out = lax.dynamic_update_slice_in_dim(out, parts[s], (me ^ s) * GROUP, 1)
    return out[None]


QORDER = (2, 4, 3, 5, 6, 7, 1, 0)
CALLS = (("open", (2, 4)), ("close", (2, 4)), ("full", (3, 5)), ("full", (6, 0)), ("full", (7, 1)))


def solution(mesh):
    split = Mesh(mesh.devices.reshape(mesh.shape["branch"], 4, 4, 2), ("branch", Z, Y, CORE))
    seq = (Z, Y, CORE)
    placed = (
        P("branch", seq, None),
        P("branch", seq, None),
        P("branch", seq, None),
        P(seq, None),
        P(seq, None),
        P(),
        P(),
        P(),
    )
    return jax.shard_map(attention, mesh=split, in_specs=placed, out_specs=P("branch", seq, None), check_vma=False)
```

```python
import math

import jax
import jax.numpy as jnp
from jax import lax
from jax.experimental import pallas as pl
from jax.experimental.pallas import tpu as pltpu
from jax.sharding import Mesh
from jax.sharding import PartitionSpec as P


KVH = 8
HD = 128
NSIB = 4
SRCMAX = 2
TOK = 128
PAST = 16
GROUP = 1024
Z, Y, CORE = "seq_0", "seq_1", "seq_2"
EXP2_SCALE = math.log2(math.e) / math.sqrt(HD)
HIDDEN = -1e30
OWN0, SIB0, DUMMY = 4, 36, 44
VROWS = HD + 16
SPAN = 4
QW = 512
HALVES = GROUP // QW
KB = SPAN * TOK


def in_hbm(array):
    return pltpu.with_memory_space_constraint(array, pltpu.HBM)


def make_kernel(kind, chunks):
    has_own, has_sib = kind != "close", kind != "open"

    def kernel(plan, *refs):
        refs = list(refs)

        def take(count):
            taken = refs[:count]
            del refs[:count]
            return taken

        queries = take(chunks)
        owns = take(4) if kind == "open" else []
        sibs = take(1) if kind == "close" else []
        states = take(chunks) if kind == "close" else []
        kbuf, vbuf = take(2) if kind != "open" else (None, None)
        outs = take(chunks)
        if kind != "full":
            kbuf, vbuf = take(2)
        todo, q_t, s_buf, p_buf, a_buf, acc, top = take(7)
        past = take(1)[0] if kind == "open" else None
        sem = take(1)[0] if kind != "full" else None
        step = pl.program_id(0)
        chunk_z, chunk_core, y = plan[0, step], plan[1, step], plan[2, step]

        def copies_in():
            pairs = []
            for r, own in enumerate(owns):
                here = pl.ds(OWN0 + 8 * r, 8)
                pairs.append((own.at[:, pl.ds(0, TOK)], kbuf.at[here]))
                pairs.append((own.at[:, pl.ds(TOK, HD)], vbuf.at[here, pl.ds(0, HD)]))
                pairs.append((own.at[:, pl.ds(TOK + HD, 2 * PAST)], past.at[r]))
            for slot in range(NSIB if sibs else 0):
                source = sibs[0].at[plan[3 + NSIB + slot, 0]]
                here = pl.ds(SIB0 + 2 * slot, 2)
                pairs.append((source.at[:, pl.ds(0, TOK)], kbuf.at[here]))
                pairs.append((source.at[:, pl.ds(TOK, HD)], vbuf.at[here, pl.ds(0, HD)]))
            return [pltpu.make_async_copy(a, b, sem.at[i]) for i, (a, b) in enumerate(pairs)]

        def begin():
            for copy in copies_in():
                copy.start()

        def fill():
            if owns:
                row = lax.broadcasted_iota(jnp.int32, (VROWS - HD, TOK), 0)
                ones = jnp.where(row == 0, 1.0, 0.0).astype(jnp.bfloat16)
                for t in range(DUMMY):
                    vbuf[t, HD:VROWS, :] = ones
                vbuf[DUMMY] = jnp.zeros((VROWS, TOK), jnp.bfloat16)
            for copy in copies_in():
                copy.wait()
            for r in range(len(owns)):
                kbuf[r] = past[r, :, 0:PAST].reshape(TOK, HD)
                vbuf[r, 0:HD] = past[r, :, PAST : 2 * PAST].reshape(TOK, HD).T
            if owns:
                kbuf[DUMMY] = kbuf[0]

        if kind != "full":
            pl.when(step == 0)(begin)

        def load(ref):
            for h in range(KVH):
                cols = slice(h * HD, (h + 1) * HD)
                scaled = ref[:, cols].T.astype(jnp.float32) * EXP2_SCALE
                upper = scaled.astype(jnp.bfloat16)
                q_t[0:HD, cols] = upper
                q_t[HD : 2 * HD, cols] = (scaled - upper.astype(jnp.float32)).astype(jnp.bfloat16)

        for i in range(chunks):

            @pl.when(step == i)
            def _(i=i):
                load(queries[i])
                if kind == "close":
                    acc[...] = states[i][0:VROWS]
                    top[...] = states[i][VROWS : VROWS + 1]

        if kind != "full":
            pl.when(step == 0)(fill)

        n = jnp.int32(0)
        if has_own:
            todo[0] = OWN0 + 2 * chunk_z + chunk_core
            for t in range(4):
                todo[1 + t] = t

            def earlier(z, n):
                for r in range(4):
                    todo[n + 2 * r] = OWN0 + 8 * r + 2 * z
                    todo[n + 2 * r + 1] = OWN0 + 8 * r + 2 * z + 1
                return n + 8

            n = lax.fori_loop(0, chunk_z, earlier, jnp.int32(5))
            todo[n] = OWN0 + 2 * chunk_z
            n = n + chunk_core
            for r in range(1, 4):
                todo[n] = OWN0 + 8 * r + 2 * chunk_z
                todo[n + 1] = OWN0 + 8 * r + 2 * chunk_z + 1
                n = n + jnp.where(y >= r, 2, 0)
        if has_sib:
            for slot in range(NSIB):
                todo[n] = SIB0 + 2 * slot
                todo[n + 1] = SIB0 + 2 * slot + 1
                n = n + jnp.where(plan[3 + slot, step] == 1, 2, 0)
        for t in range(2 * SPAN):
            todo[n + t] = DUMMY
        groups = lax.div(n + SPAN - 1, SPAN)

        def score(j, g):
            keys = jnp.concatenate([kbuf[todo[j * SPAN + t]] for t in range(SPAN)], axis=0)
            s_buf[g] = lax.dot_general(
                jnp.concatenate([keys, keys], axis=1),
                q_t[:, g * QW : (g + 1) * QW],
                (((1,), (0,)), ((), ())),
                preferred_element_type=jnp.float32,
            )

        def weigh(g, first=False):
            cols = slice(g * QW, (g + 1) * QW)
            s = s_buf[g]
            if first:
                key = lax.broadcasted_iota(jnp.int32, (TOK, QW), 0)
                token = lax.broadcasted_iota(jnp.int32, (TOK, QW), 1) % TOK
                s = jnp.concatenate([jnp.where(key <= token, s[0:TOK], HIDDEN), s[TOK:]], axis=0)
            peak = jnp.max(s, axis=0, keepdims=True)
            if not first:
                before = top[:, cols]
                peak = jnp.maximum(before, peak)
                a_buf[:, cols] = jnp.exp2(before - peak)
            top[:, cols] = peak
            p_buf[g] = jnp.exp2(s - peak).astype(jnp.bfloat16)

        def gather(j, g, first=False):
            cols = slice(g * QW, (g + 1) * QW)
            values_t = jnp.concatenate([vbuf[todo[j * SPAN + t]] for t in range(SPAN)], axis=1)
            part = lax.dot_general(
                values_t, p_buf[g], (((1,), (0,)), ((), ())), preferred_element_type=jnp.float32
            )
            acc[:, cols] = part if first else acc[:, cols] * a_buf[:, cols] + part

        last = HALVES - 1

        def turn(j, carry):
            for g in range(HALVES):
                if g == 0:
                    gather(j - 1, last)
                else:
                    gather(j, g - 1)
                weigh(g)
                if g < last:
                    score(j, g + 1)
                else:
                    score(j + 1, 0)
            return carry

        if has_own:
            score(0, 0)
            for g in range(HALVES):
                if g < last:
                    score(0, g + 1)
                else:
                    score(1, 0)
                if g:
                    gather(0, g - 1, first=True)
                weigh(g, first=True)
            acc[:, last * QW :] = jnp.zeros((VROWS, QW), jnp.float32)
            a_buf[:, last * QW :] = jnp.ones((1, QW), jnp.float32)
            lax.fori_loop(1, groups, turn, 0)
            gather(groups - 1, last)
        else:
            def listed(j, carry):
                for g in range(HALVES):
                    score(j, g)
                for g in range(HALVES):
                    weigh(g)
                    gather(j, g)
                return carry

            lax.fori_loop(0, groups, listed, 0)

        def store(ref):
            if kind == "open":
                ref[0:VROWS] = acc[...]
                ref[VROWS:] = jnp.broadcast_to(top[...], (8, GROUP))
                return
            for h in range(KVH):
                cols = slice(h * HD, (h + 1) * HD)
                ref[:, cols] = (acc[0:HD, cols] / acc[HD : HD + 1, cols]).T.astype(jnp.bfloat16)

        for i in range(chunks):

            @pl.when(step == i)
            def _(i=i):
                store(outs[i])

    return kernel


def attend(kind, plan, queries, states, source, buffers):
    chunks = len(queries)

    def whole(a):
        return pl.BlockSpec(a.shape, lambda i, plan: (0,) * a.ndim, pipeline_mode=pl.Buffered(1))

    blocked = list(queries)
    states = states if kind == "close" else []
    raw = list(source) if kind != "full" else []
    kept = [*states, *buffers] if kind != "open" else []
    if kind == "open":
        result = jax.ShapeDtypeStruct((VROWS + 8, GROUP), jnp.float32)
    else:
        result = jax.ShapeDtypeStruct((TOK, GROUP), jnp.bfloat16)
    tile_shapes = [(DUMMY + 1, TOK, HD), (DUMMY + 1, VROWS, TOK)]
    tiles = [jax.ShapeDtypeStruct(shape, jnp.bfloat16) for shape in tile_shapes] if kind != "full" else []
    resident = pl.BlockSpec(memory_space=pltpu.VMEM)
    scratch = [
        pltpu.SMEM((72,), jnp.int32),
        pltpu.VMEM((2 * HD, GROUP), jnp.bfloat16),
        pltpu.VMEM((HALVES, KB, QW), jnp.float32),
        pltpu.VMEM((HALVES, KB, QW), jnp.bfloat16),
        pltpu.VMEM((1, GROUP), jnp.float32),
        pltpu.VMEM((VROWS, GROUP), jnp.float32),
        pltpu.VMEM((1, GROUP), jnp.float32),
    ]
    if kind == "open":
        scratch.append(pltpu.VMEM((4, 8, 2 * PAST, HD), jnp.bfloat16))
    if kind != "full":
        scratch.append(pltpu.SemaphoreType.DMA((16,)))
    first_kept = 1 + len(blocked) + len(raw) + len(states)
    aliases = {first_kept: chunks, first_kept + 1: chunks + 1} if kind == "close" else {}
    return pl.pallas_call(
        make_kernel(kind, chunks),
        out_shape=(result,) * chunks + tuple(tiles),
        grid_spec=pltpu.PrefetchScalarGridSpec(
            num_scalar_prefetch=1,
            grid=(chunks,),
            in_specs=[whole(a) for a in blocked]
            + [pl.BlockSpec(memory_space=pltpu.HBM)] * len(raw)
            + [resident] * len(kept),
            out_specs=[resident if kind == "open" else pl.BlockSpec(result.shape, lambda i, plan: (0, 0))] * chunks
            + [resident] * len(tiles),
            scratch_shapes=scratch,
        ),
        input_output_aliases=aliases,
        compiler_params=pltpu.CompilerParams(vmem_limit_bytes=24 * 2**20),
    )(plan, *[in_hbm(a) for a in blocked], *[in_hbm(a) for a in raw], *kept)


def shifted(value, axis, by):
    n = lax.axis_size(axis)
    return lax.ppermute(value, axis, [(k, (k + by) % n) for k in range(n)])


def exchanged(value, step):
    return lax.ppermute(value, (Z, CORE), [(k, k ^ step) for k in range(8)])


def after(value, *others):
    return lax.optimization_barrier((value, *others))[0]


def packing(key_ref, value_ref, past_key_ref, past_value_ref, out_ref):
    for h in range(KVH):
        cols = slice(h * HD, (h + 1) * HD)
        out_ref[h, 0:TOK] = key_ref[0, :, cols]
        out_ref[h, TOK : TOK + HD] = value_ref[0, :, cols].T
        out_ref[h, TOK + HD : TOK + HD + PAST] = past_key_ref[:, cols]
        out_ref[h, TOK + HD + PAST :] = past_value_ref[:, cols]


def packed(*arrays):
    shape = jax.ShapeDtypeStruct((KVH, TOK + HD + 2 * PAST, HD), jnp.bfloat16)
    return pl.pallas_call(packing, out_shape=shape, name="packing")(*arrays)


def picking(where, own0, own1, own2, own3, out_ref, sem):
    count = out_ref.shape[0]

    def copy(own, e):
        pair = own.at[pl.ds(2 * where[count + e], 2), pl.ds(0, TOK + HD)]
        return pltpu.make_async_copy(pair, out_ref.at[e], sem.at[e])

    for e in range(count):
        for r, own in enumerate((own0, own1, own2, own3)):

            @pl.when(where[e] == r)
            def _(own=own, e=e):
                copy(own, e).start()

    for e in range(count):
        copy(own0, e).wait()


def picked(where, owns):
    entries = where.shape[0] // 2
    shape = (entries, 2, TOK + HD, HD)
    return pl.pallas_call(
        picking,
        out_shape=jax.ShapeDtypeStruct(shape, jnp.bfloat16),
        grid_spec=pltpu.PrefetchScalarGridSpec(
            num_scalar_prefetch=1,
            grid=(1,),
            in_specs=[pl.BlockSpec(memory_space=pltpu.HBM)] * 4,
            out_specs=pl.BlockSpec(shape, lambda i, where: (0, 0, 0, 0), pipeline_mode=pl.Buffered(1)),
            scratch_shapes=[pltpu.SemaphoreType.DMA((entries,))],
        ),
        compiler_params=pltpu.CompilerParams(vmem_limit_bytes=16 * 2**20),
        name="picking",
    )(where, *[in_hbm(own) for own in owns])


def attention(query, key_new, value_new, hist_key, hist_value, sib_source, sib_block, sib_mask):
    z, y, core = lax.axis_index(Z), lax.axis_index(Y), lax.axis_index(CORE)
    me = z * 2 + core
    reader = lax.axis_index("branch")

    send = packed(key_new, value_new, hist_key, hist_value)
    own = lax.all_to_all(send, (Z, CORE), split_axis=0, concat_axis=0, tiled=True)
    my_source = lax.dynamic_index_in_dim(sib_source, reader, 0, keepdims=False)
    my_mask = lax.dynamic_index_in_dim(sib_mask, reader, 0, keepdims=False)
    from_me = sib_source == reader
    sender_rank = jnp.cumsum(from_me.astype(jnp.int32), axis=1) - 1
    slot_hit = from_me[:, :, None] & (
        sender_rank[:, :, None] == jnp.arange(SRCMAX, dtype=jnp.int32)[None, None, :]
    )
    send_table = jnp.sum(jnp.where(slot_hit, sib_block[:, :, None], 0), axis=1).reshape(-1)
    where = jnp.concatenate([(y - send_table) % 4, send_table // 4]).astype(jnp.int32)
    slots = jnp.arange(NSIB, dtype=jnp.int32)
    same = (my_source[None, :] == my_source[:, None]) & (slots[None, :] < slots[:, None])
    rank = jnp.sum(same.astype(jnp.int32), axis=1)
    flat = (my_source * SRCMAX + rank).astype(jnp.int32)

    def plan_of(steps):
        chunks = jnp.stack([me ^ s for s in steps])
        visible = my_mask[(chunks // 2) * 4 + y]
        rows = [(chunks // 2)[None], (chunks % 2)[None], jnp.broadcast_to(y, (1, len(steps))), visible.T]
        rows.append(jnp.broadcast_to(flat[:, None], (NSIB, len(steps))))
        return jnp.concatenate(rows, axis=0).astype(jnp.int32)

    plans = [plan_of(steps) for _, steps in CALLS]
    own, where, *plans = lax.optimization_barrier((own, where, *plans))
    up, down = shifted(own, Y, 1), shifted(own, Y, -1)
    onward = shifted(up[:4], Y, 1), shifted(down[4:], Y, -1)
    over = jnp.concatenate(onward, axis=0)
    owns = (own, up, over, down)

    cols = after(query[0], own)
    queries = {}
    for s in QORDER:
        piece = lax.dynamic_slice_in_dim(cols, (me ^ s) * GROUP, GROUP, 1)
        queries[s] = exchanged(piece, s) if s else piece

    sent = picked(where, owns)
    sib = lax.all_to_all(sent, "branch", split_axis=0, concat_axis=0, tiled=True)
    parts, states, previous, buffers = {}, {}, None, ()
    for number, (kind, steps) in enumerate(CALLS):
        asked = [queries[s] for s in steps]
        if previous is not None:
            asked[0] = after(asked[0], previous)
        source = owns if kind == "open" else (sib,)
        results = attend(kind, plans[number], asked, [states.get(s) for s in steps], source, buffers)
        if kind != "full":
            buffers = results[len(steps) :]
        previous = results[0]
        for s, result in zip(steps, results):
            if kind == "open":
                states[s] = result
            else:
                parts[s] = exchanged(result, s) if s else result
    out = jnp.zeros((TOK, KVH * GROUP), jnp.bfloat16)
    for s in range(8):
        out = lax.dynamic_update_slice_in_dim(out, parts[s], (me ^ s) * GROUP, 1)
    return out[None]


QORDER = (2, 4, 3, 5, 6, 7, 1, 0)
CALLS = (("open", (2, 4)), ("close", (2, 4)), ("full", (3, 5)), ("full", (6, 0)), ("full", (7, 1)))


def solution(mesh):
    split = Mesh(mesh.devices.reshape(mesh.shape["branch"], 4, 4, 2), ("branch", Z, Y, CORE))
    seq = (Z, Y, CORE)
    placed = (
        P("branch", seq, None),
        P("branch", seq, None),
        P("branch", seq, None),
        P(seq, None),
        P(seq, None),
        P(),
        P(),
        P(),
    )
    return jax.shard_map(attention, mesh=split, in_specs=placed, out_specs=P("branch", seq, None), check_vma=False)
```
